32 devices in a mesh: side: 2 (over x), row: 4 (over z), col: 4 (over y, core).
Axes of the slice: x: 2, y: 2, z: 4, core: 2. Of those that a mesh axis runs over, the one named last changes fastest.
Arguments:
- old_vectors: bfloat16 [2, 32768, 16384], P('side', 'row', 'col'), may hold values from -6 to 6
- reflectors: bfloat16 [2, 2, 32768, 512], P('side', None, 'row', 'col'), may hold values from -0.0625 to 0.0625
- triangles: float32 [2, 2, 512, 512], P('side'), may hold values from -0.25 to 0.25
- pole_sq: float32 [32768], replicated, may hold values from 1 to 65536, as said below
- coupling: float32 [32768], replicated, may hold values from -1 to 1
- deflated: int32 [32768], replicated, may hold values 0 or 1
- pole_order: int32 [32768], replicated, may hold values from 0 to 32767, each once
- anchors: int32 [1024], replicated, may hold values from 0 to 32766, as said below
- root_fraction: float32 [1024], replicated, may hold values from 0.2 to 0.8
Outputs:
- vectors: bfloat16 [2, 1024, 32768], P('side', 'col', 'row')
The draws below stay inside these ranges and needn't reach their ends.
Inputs may be any that keep to these rules, and one draw needn't show every extreme that they name: `pole_sq`: strictly increasing; successive entries differ by 0.5 or more. `anchors`: distinct entries.
All inputs are finite; a program needn't handle non-finite values.
Results may differ from the reference program's by a relative error of at most 0.014.
Values may be sent and summed in bfloat16 or wider, within the bound.
No kernel may reach another device: no remote copies, remote signals or barrier semaphores. Data moves between devices by JAX's collectives and lax.ppermute only.
A program may use at most 192 MiB of HBM per device.

```python
import jax
import jax.numpy as jnp
from jax import lax

M = 32768
K = 1024
B = 512
P_SIZE = 2


def draw_pole_sq(key, part):
    pole_gaps = jax.random.uniform(jax.random.fold_in(key, 11), (M,), jnp.float32, 0.5, 2.0)
    return 1.0 + jnp.cumsum(pole_gaps) - pole_gaps[0]


def draw_anchors(key, part):
    interior = jax.random.permutation(jax.random.fold_in(key, 21), M - 3)[:K - 2] + 1
    ends_first = jnp.concatenate([jnp.array([0, M - 2], jnp.int32), interior.astype(jnp.int32)])
    return ends_first[jax.random.permutation(jax.random.fold_in(key, 22), K)]


def plant(entries, stream_key, smallest, high):
    spot = [jax.random.randint(jax.random.fold_in(stream_key, axis), (), 0, length) for axis, length in enumerate(entries.shape)]
    widest = entries.shape.index(max(entries.shape))
    beside = spot[:widest] + [(spot[widest] + 1) % entries.shape[widest]] + spot[widest + 1:]
    return entries.at[tuple(spot)].set(smallest).at[tuple(beside)].set(high)


def levels(rng, extent, shards, low, high):
    factor_of, own = 1.0, jax.random.fold_in(rng, 6)
    for dim, blocks in shards:
        steps = jnp.exp(jax.random.uniform(jax.random.fold_in(own, dim), (blocks,), jnp.float32, low / len(shards), high / len(shards)))
        factor_of = factor_of * jnp.repeat(steps, extent[dim] // blocks).reshape([-1 if axis == dim else 1 for axis in range(len(extent))])
    return factor_of


def gaussian(stream_key, extent, scale, reach, shards=(), kind=jnp.bfloat16):
    entries = scale * jax.random.normal(stream_key, extent, jnp.float32)
    if shards:
        entries = entries * levels(stream_key, extent, shards, -0.22, 0.18)
    return jnp.clip(entries, -reach, reach).astype(kind)


def setup_inputs(seed: int = 0) -> dict:
    splits = jax.random.split(jax.random.key(seed), 10)
    return {
        "old_vectors": gaussian(splits[0], (2, M, M // 2), 1.0, 6.0, ((0, 2), (1, 4), (2, 4))),
        "reflectors": gaussian(splits[1], (2, P_SIZE, M, B), (M // 4) ** -0.5, 0.0625, ((0, 2), (2, 4), (3, 4))),
        "triangles": gaussian(splits[2], (2, P_SIZE, B, B), B ** -0.5, 0.25, ((0, 2),), jnp.float32),
        "pole_sq": draw_pole_sq(jax.random.fold_in(splits[9], 71), 0),
        "coupling": jnp.clip(jax.random.uniform(splits[4], (M,), jnp.float32, -1.0, 1.0), -1.0, 1.0),
        "deflated": plant((jax.random.randint(splits[5], (M,), 0, 4) < 1).astype(jnp.int32), jax.random.fold_in(splits[5], 1), 0, 1),
        "pole_order": jax.random.permutation(splits[6], M).astype(jnp.int32),
        "anchors": draw_anchors(jax.random.fold_in(splits[9], 71), 0),
        "root_fraction": jnp.clip(jax.random.uniform(splits[8], (K,), jnp.float32, 0.2, 0.8), 0.2, 0.8),
    }


def reference(old_vectors, reflectors, triangles, pole_sq, coupling, deflated, pole_order, anchors, root_fraction):
    half_order = old_vectors.shape[2]
    anchor_sq = pole_sq[anchors]
    pole_gap = pole_sq[anchors + 1] - anchor_sq
    dead_triplet = deflated[anchors] == 1
    target = pole_order[anchors]
    live_pole = (1 - deflated).astype(pole_sq.dtype)
    denom = pole_sq[:, None] - anchor_sq[None, :] - root_fraction[None, :] * pole_gap[None, :]
    results = []
    for side_index in range(2):
        weight = jnp.ones_like(pole_sq) if side_index == 0 else jnp.sqrt(pole_sq)
        secular = (live_pole * coupling * weight)[:, None] / denom
        squares = lax.optimization_barrier(jnp.sum(secular * secular, axis=0))
        col_scale = jnp.where(dead_triplet, jnp.ones_like(squares), 1.0 / jnp.sqrt(squares + 1e-06))
        placed = jnp.zeros_like(secular).at[pole_order].set(secular)
        onehot = (jnp.arange(2 * half_order, dtype=jnp.int32)[:, None] == target[None, :]).astype(secular.dtype)
        mixing = jnp.where(dead_triplet[None, :], onehot, placed).astype(jnp.bfloat16)
        upper_part = jnp.dot(old_vectors[side_index, :half_order], mixing[:half_order], preferred_element_type=jnp.float32)
        lower_part = jnp.dot(old_vectors[side_index, half_order:], mixing[half_order:], preferred_element_type=jnp.float32)
        current = jnp.concatenate([upper_part, lower_part], axis=0).T * col_scale[:, None]
        for panel_index in reversed(range(P_SIZE)):
            panel_rows = reflectors[side_index, panel_index]
            current_low = current.astype(jnp.bfloat16)
            projected = jnp.dot(current_low, panel_rows, preferred_element_type=jnp.float32)
            upper_tri = jnp.triu(triangles[side_index, panel_index])
            coefficients = jnp.dot(projected, upper_tri.T, precision=lax.Precision.HIGHEST).astype(jnp.bfloat16)
            current = current - jnp.dot(coefficients, panel_rows.T, preferred_element_type=jnp.float32)
        results.append(current.astype(jnp.bfloat16))
    return jnp.stack(results)
```

```python
import jax
import jax.numpy as jnp
from jax import lax
from jax.experimental import pallas as pl
from jax.experimental.pallas import tpu as pltpu
from jax.sharding import PartitionSpec as P


LANES = 128
HIGHEST = lax.Precision.HIGHEST
NT = (((1,), (1,)), ((), ()))
TN = (((0,), (0,)), ((), ()))


def tile_of(size, want):
    tile = min(size, want)
    while size % tile:
        tile //= 2
    return tile


def split3(x):
    first = x.astype(jnp.bfloat16).astype(jnp.float32)
    rest = x - first
    second = rest.astype(jnp.bfloat16).astype(jnp.float32)
    return first, second, rest - second


def add_up(step, total_ref, value):
    @pl.when(step == 0)
    def _():
        total_ref[...] = value

    @pl.when(step > 0)
    def _():
        total_ref[...] += value


def column_kernel(place_ref, order_ref, sq_ref, coupling_ref, deflated_ref, out_sq_ref, out_num_ref, acc_ref):
    step = pl.program_id(0)

    rows = out_sq_ref.shape[0]
    chunk = order_ref.shape[1]
    local = order_ref[...] - place_ref[0]
    high = jnp.broadcast_to(local >> 7, (rows, chunk))
    low = jnp.broadcast_to(local & 127, (LANES, chunk))
    in_row = high == lax.broadcasted_iota(jnp.int32, (rows, chunk), 0)
    in_lane = jnp.where(low == lax.broadcasted_iota(jnp.int32, (LANES, chunk), 0), 1.0, 0.0)
    num = (1 - deflated_ref[...]).astype(jnp.float32) * coupling_ref[...]
    parts = [
        jnp.where(in_row, jnp.broadcast_to(part, (rows, chunk)), 0.0).astype(jnp.bfloat16)
        for part in split3(sq_ref[...]) + split3(num)
    ]
    add_up(
        step,
        acc_ref,
        lax.dot_general(
            jnp.concatenate(parts, axis=0),
            in_lane.astype(jnp.bfloat16),
            NT,
            preferred_element_type=jnp.float32,
        ),
    )

    @pl.when(step == pl.num_programs(0) - 1)
    def _():
        picked = [acc_ref[i * rows : (i + 1) * rows] for i in range(6)]
        col_sq = (picked[0] + picked[1]) + picked[2]
        weight = jnp.where(place_ref[1] == 0, jnp.ones_like(col_sq), jnp.sqrt(col_sq))
        out_sq_ref[...] = col_sq
        out_num_ref[...] = ((picked[3] + picked[4]) + picked[5]) * weight


def column_tables(place, pole_order, pole_sq, coupling, deflated, col_width):
    order_size = pole_order.shape[0]
    rows = col_width // LANES
    chunk = tile_of(order_size, 4096)
    row_spec = pl.BlockSpec((1, chunk), lambda i, place: (0, i))
    out_spec = pl.BlockSpec((rows, LANES), lambda i, place: (0, 0))
    return pl.pallas_call(
        column_kernel,
        grid_spec=pltpu.PrefetchScalarGridSpec(
            num_scalar_prefetch=1,
            grid=(order_size // chunk,),
            in_specs=[row_spec] * 4,
            out_specs=[out_spec] * 2,
            scratch_shapes=[pltpu.VMEM((6 * rows, LANES), jnp.float32)],
        ),
        out_shape=[jax.ShapeDtypeStruct((rows, LANES), jnp.float32)] * 2,
        name="columns",
    )(place, *(x.reshape(1, order_size) for x in (pole_order, pole_sq, coupling, deflated)))


def down(row, height=LANES):
    return jnp.broadcast_to(row, (height, row.shape[1])).T


def mixing_kernel(place_ref, anchors_ref, fraction_ref, pole_ref, deflated_ref, order_ref, sq_ref, num_ref,
                  mix_ref, squares_ref, dead_ref):
    count = anchors_ref.shape[2]
    anchor = anchors_ref[0]

    def lookup(index, tables):
        table_rows = tables.shape[0]
        onehot = jnp.where(
            lax.broadcasted_iota(jnp.int32, (table_rows, count), 0)
            == jnp.broadcast_to(index >> 7, (table_rows, count)),
            1.0,
            0.0,
        )
        found = lax.dot_general(tables, onehot, TN, precision=HIGHEST, preferred_element_type=jnp.float32)
        mask = lax.broadcasted_iota(jnp.int32, (LANES, count), 0) == jnp.broadcast_to(index & 127, (LANES, count))
        return [
            jnp.sum(jnp.where(mask, found[i : i + LANES], 0.0), axis=0, keepdims=True)
            for i in range(0, found.shape[0], LANES)
        ]

    poles = pole_ref[...]
    tables = jnp.concatenate(
        [poles, deflated_ref[...].astype(jnp.float32), order_ref[...].astype(jnp.float32)], axis=1
    )
    anchor_sq, dead, target = lookup(anchor, tables)
    (next_sq,) = lookup(anchor + 1, poles)
    dead_ref[0] = dead
    anchor_col = down(anchor_sq)
    shift_col = down(fraction_ref[0] * (next_sq - anchor_sq))
    dead_col = down(dead)
    target_col = down(target - place_ref[0].astype(jnp.float32))
    block = tile_of(count, 64)
    chunks = sq_ref.shape[0]
    sums = []
    for start in range(0, count, block):
        part = slice(start, start + block)
        base, shift = anchor_col[part], shift_col[part]
        is_dead, goal = dead_col[part] > 0.5, target_col[part]
        lane = lax.broadcasted_iota(jnp.int32, (block, LANES), 1).astype(jnp.float32)

        def body(c, total, part=part, base=base, shift=shift, is_dead=is_dead, goal=goal, lane=lane):
            col_sq = sq_ref[pl.ds(c, 1), :]
            den = (col_sq - base) - shift
            secular = num_ref[pl.ds(c, 1), :] / den
            first = c * LANES
            onehot = jnp.where(lane + first.astype(jnp.float32) == goal, 1.0, 0.0)
            mix_ref[part, pl.ds(pl.multiple_of(first, LANES), LANES)] = jnp.where(is_dead, onehot, secular).astype(
                jnp.bfloat16
            )
            return total + secular * secular

        sums.append(lax.fori_loop(0, chunks, body, jnp.zeros((block, LANES), jnp.float32), unroll=2))
    total = jnp.concatenate(sums, axis=0)
    squares_ref[0] = jnp.sum(total.T, axis=0, keepdims=True)


def mixing_rows(place, col_index, slots, anchors3, fraction3, tables, col_tables):
    count = anchors3.shape[2]
    rows = col_tables[0].shape[0]
    width = rows * LANES
    scalars = jnp.concatenate([place, jnp.asarray(slots, jnp.int32) ^ col_index])

    def pick(i, sc):
        return (sc[2 + i], 0, 0)

    row_spec = pl.BlockSpec((1, 1, count), pick)
    whole = lambda a: pl.BlockSpec(a.shape, lambda i, sc: (0,) * a.ndim)
    out_row = pl.BlockSpec((1, 1, count), lambda i, sc: (i, 0, 0))
    return pl.pallas_call(
        mixing_kernel,
        grid_spec=pltpu.PrefetchScalarGridSpec(
            num_scalar_prefetch=1,
            grid=(len(slots),),
            in_specs=[row_spec, row_spec] + [whole(t) for t in tables] + [whole(t) for t in col_tables],
            out_specs=[pl.BlockSpec((count, width), lambda i, sc: (i, 0)), out_row, out_row],
        ),
        out_shape=[
            jax.ShapeDtypeStruct((len(slots) * count, width), jnp.bfloat16),
            jax.ShapeDtypeStruct((len(slots), 1, count), jnp.float32),
            jax.ShapeDtypeStruct((len(slots), 1, count), jnp.float32),
        ],
        name="mixing",
    )(scalars, anchors3, fraction3, *tables, *col_tables)


def merge(mix, old, start, size, kept):
    total, depth = mix.shape
    rows = tile_of(size, 512)
    sent = total - kept[0] - kept[1]
    splits = [(0, sent), (sent, kept[0]), (sent + kept[0], kept[1])]
    first = start // rows

    def kernel(mix_ref, old_ref, *outs):
        value = lax.dot_general(mix_ref[...], old_ref[...], NT, preferred_element_type=jnp.float32)
        for (at, length), out in zip(splits, outs):
            out[...] = value[at : at + length].astype(jnp.bfloat16)

    return pl.pallas_call(
        kernel,
        grid=(size // rows,),
        in_specs=[
            pl.BlockSpec((total, depth), lambda i: (0, 0), pipeline_mode=pl.Buffered(1)),
            pl.BlockSpec((rows, depth), lambda i: (first + i, 0)),
        ],
        out_specs=[pl.BlockSpec((length, rows), lambda i: (0, i)) for _, length in splits],
        out_shape=[jax.ShapeDtypeStruct((length, size), jnp.bfloat16) for _, length in splits],
        name="merge",
    )(mix, old)


def ranges(parts, tile):
    found, at = [], 0
    for part in parts:
        found.append((at, part // tile))
        at += part // tile
    return found, at


def block_spec(height, tile, at, steps, row=0, lane=0):
    return pl.BlockSpec((height, tile), lambda i, sc: (row, lane + jnp.clip(i - at, 0, steps - 1)))


def project(place, parts, start, pieces, row_count, init=None, last=True):
    slots, (panels, _, wide) = len(pieces), pieces[0].shape
    count = parts[0][0].shape[0]
    order = slots * wide
    tile = tile_of(parts[0][0].shape[1], 1024)
    spans, steps = ranges([part[0].shape[1] for part in parts], tile)
    sub = count // row_count
    first = start // tile
    n_init = 0 if init is None else 1

    def kernel(sc_ref, *refs):
        part_refs, refs = refs[: 3 * len(parts)], refs[3 * len(parts) :]
        piece_refs, refs = refs[:slots], refs[slots:]
        init_refs, refs = refs[:n_init], refs[n_init:]
        outs, acc_ref = refs[:-1], refs[-1]
        step = pl.program_id(0)
        for n, (at, length) in enumerate(spans):
            far_ref, own_ref, sent_ref = part_refs[3 * n : 3 * n + 3]

            @pl.when((step >= at) & (step < at + length))
            def _(far_ref=far_ref, own_ref=own_ref, sent_ref=sent_ref):
                own = own_ref[...].astype(jnp.float32) + sent_ref[...].astype(jnp.float32)
                both = jnp.concatenate([far_ref[...], own.astype(jnp.bfloat16)], axis=0)
                for p in range(panels):
                    panel = jnp.concatenate([piece_refs[k][p] for k in range(slots)], axis=1)
                    value = jnp.dot(both, panel, preferred_element_type=jnp.float32)
                    if init is None:
                        add_up(step, acc_ref.at[p], value)
                    else:

                        @pl.when(step == 0)
                        def _(p=p, value=value):
                            acc_ref[p] = init_refs[0][p] + value

                        @pl.when(step > 0)
                        def _(p=p, value=value):
                            acc_ref[p] += value

        @pl.when(step == pl.num_programs(0) - 1)
        def _():
            if not last:
                outs[0][...] = acc_ref[...]
                return
            col, row = sc_ref[0], sc_ref[1]
            for t in range(row_count):
                at = pl.multiple_of((row ^ t) * sub, sub)
                for p in range(panels):
                    for k in range(slots):
                        lanes = pl.ds(pl.multiple_of(p * order + (col ^ k) * wide, wide), wide)
                        cols = slice(k * wide, (k + 1) * wide)
                        outs[0][t, :, lanes] = acc_ref[p, pl.ds(at, sub), cols].astype(jnp.bfloat16)
                        outs[1][t, :, lanes] = acc_ref[p, pl.ds(at + count, sub), cols].astype(jnp.bfloat16)

    acc_shape = (panels, 2 * count, order)
    if last:
        out_shapes = [jax.ShapeDtypeStruct((row_count, sub, panels * order), jnp.bfloat16)] * 2
    else:
        out_shapes = [jax.ShapeDtypeStruct(acc_shape, jnp.float32)]
    in_specs = []
    for at, length in spans:
        in_specs += [block_spec(count, tile, at, length)] * 2 + [block_spec(count, tile, at, length, row=1)]
    in_specs += [pl.BlockSpec((panels, tile, wide), lambda i, sc: (0, first + i, 0))] * slots
    if init is not None:
        in_specs += [pl.BlockSpec(acc_shape, lambda i, sc: (0, 0, 0), pipeline_mode=pl.Buffered(1))]
    return pl.pallas_call(
        kernel,
        grid_spec=pltpu.PrefetchScalarGridSpec(
            num_scalar_prefetch=1,
            grid=(steps,),
            in_specs=in_specs,
            out_specs=[pl.BlockSpec(s.shape, lambda i, sc: (0, 0, 0)) for s in out_shapes],
            scratch_shapes=[pltpu.VMEM(acc_shape, jnp.float32)],
        ),
        out_shape=out_shapes,
        name="project",
    )(place, *(a for part in parts for a in part), *pieces, *(() if init is None else (init,)))


def panel_products(place, pieces, row_count, pairs):
    slots, (panels, size, wide) = len(pieces), pieces[0].shape
    order = slots * wide
    tile = tile_of(size, 2048)
    sub_gram = order // row_count

    def kernel(sc_ref, *refs):
        piece_refs, (gram_out, gram_ref, nat_ref) = refs[:slots], refs[slots:]
        step = pl.program_id(0)
        for n, (later, earlier) in enumerate(pairs):
            panel = jnp.concatenate([piece_refs[k][later] for k in range(slots)], axis=1)
            product = lax.dot_general(
                panel, piece_refs[0][earlier], TN, preferred_element_type=jnp.float32
            )
            add_up(step, gram_ref.at[n], product)

        @pl.when(step == pl.num_programs(0) - 1)
        def _():
            col, row = sc_ref[0], sc_ref[1]
            for n in range(len(pairs)):
                for k in range(slots):
                    at = pl.multiple_of((col ^ k) * wide, wide)
                    nat_ref[pl.ds(at, wide), :] = gram_ref[n, k * wide : (k + 1) * wide, :]
                for t in range(row_count):
                    at = pl.multiple_of((row ^ t) * sub_gram, sub_gram)
                    gram_out[t, n] = nat_ref[pl.ds(at, sub_gram), :].astype(jnp.bfloat16)

    out_shape = jax.ShapeDtypeStruct((row_count, len(pairs), sub_gram, wide), jnp.bfloat16)
    return pl.pallas_call(
        kernel,
        grid_spec=pltpu.PrefetchScalarGridSpec(
            num_scalar_prefetch=1,
            grid=(size // tile,),
            in_specs=[pl.BlockSpec((panels, tile, wide), lambda i, sc: (0, i, 0))] * slots,
            out_specs=pl.BlockSpec(out_shape.shape, lambda i, sc: (0, 0, 0, 0)),
            scratch_shapes=[
                pltpu.VMEM((len(pairs), order, wide), jnp.float32),
                pltpu.VMEM((order, wide), jnp.float32),
            ],
        ),
        out_shape=out_shape,
        name="gram",
    )(place, *pieces)


def coefficients(place, shares, grams, triangles, pairs):
    panels, order = triangles.shape[0], triangles.shape[1]
    sub = shares[0].shape[0]
    slots = len(grams)
    row_count, _, sub_gram, wide = grams[0].shape

    def kernel(sc_ref, *refs):
        share_refs = refs[: len(shares)]
        gram_refs = refs[len(shares) : len(shares) + slots]
        tri_ref, out_ref, nat_ref = refs[len(shares) + slots :]
        col, row = sc_ref[0], sc_ref[1]
        for n in range(len(pairs)):
            for k in range(slots):
                for t in range(row_count):
                    rows = pl.ds(pl.multiple_of((row ^ t) * sub_gram, sub_gram), sub_gram)
                    lanes = pl.ds(pl.multiple_of((col ^ k) * wide, wide), wide)
                    nat_ref[n, rows, lanes] = gram_refs[k][t, n].astype(jnp.float32)
        total = share_refs[0][...].astype(jnp.float32)
        for ref in share_refs[1:]:
            total = total + ref[...].astype(jnp.float32)
        keep = lax.broadcasted_iota(jnp.int32, (order, order), 0) <= lax.broadcasted_iota(
            jnp.int32, (order, order), 1
        )
        found = [None] * panels
        for p in reversed(range(panels)):
            projected = total[:, p * order : (p + 1) * order]
            for later in range(p + 1, panels):
                gram = nat_ref[pairs.index((later, p))].astype(jnp.bfloat16)
                projected = projected - jnp.dot(found[later], gram, preferred_element_type=jnp.float32)
            upper = jnp.where(keep, tri_ref[p], 0.0)
            found[p] = lax.dot_general(
                projected, upper, NT, precision=HIGHEST, preferred_element_type=jnp.float32
            ).astype(jnp.bfloat16)
            out_ref[:, p * order : (p + 1) * order] = found[p]

    whole = lambda a: pl.BlockSpec(a.shape, lambda i, sc: (0,) * a.ndim)
    args = [*shares, *grams, triangles]
    return pl.pallas_call(
        kernel,
        grid_spec=pltpu.PrefetchScalarGridSpec(
            num_scalar_prefetch=1,
            grid=(1,),
            in_specs=[whole(a) for a in args],
            out_specs=pl.BlockSpec((sub, panels * order), lambda i, sc: (0, 0)),
            scratch_shapes=[pltpu.VMEM((len(pairs), order, order), jnp.float32)],
        ),
        out_shape=jax.ShapeDtypeStruct((sub, panels * order), jnp.bfloat16),
        name="coefficients",
    )(place, *args)


def finish(place, parts, start, pieces, coefs, scales, partial=None):
    slots, (panels, total_rows, wide) = len(pieces), pieces[0].shape
    count = parts[0][0].shape[0]
    order = slots * wide
    leads = partial is None
    tile = min([tile_of(part[2].shape[1], 1024) for part in parts])
    spans, steps = ranges([part[2].shape[1] for part in parts], tile)
    first = start // tile
    n_coef, n_scale = len(coefs), len(scales)

    def kernel(sc_ref, *refs):
        part_refs, refs = refs[: 3 * len(parts)], refs[3 * len(parts) :]
        piece_refs, refs = refs[:slots], refs[slots:]
        coef_refs, refs = refs[:n_coef], refs[n_coef:]
        scale_refs, refs = refs[:n_scale], refs[n_scale:]
        if leads:
            out_ref, coef_ref, scale_ref, wide_ref = refs
        else:
            out_ref, coef_ref, scale_ref = refs[1], coef_refs[0], scale_refs[0]
        step = pl.program_id(0)

        if leads:

            @pl.when(step == 0)
            def _():
                col, row = sc_ref[0], sc_ref[1]
                sub = coef_refs[0].shape[0]
                for t in range(n_coef):
                    rows = pl.ds(pl.multiple_of((row ^ t) * sub, sub), sub)
                    for p in range(panels):
                        for k in range(slots):
                            lanes = pl.ds(pl.multiple_of(p * order + (col ^ k) * wide, wide), wide)
                            at = p * order + k * wide
                            wide_ref[rows, at : at + wide] = coef_refs[t][:, lanes].astype(jnp.float32)
                coef_ref[...] = wide_ref[...].astype(jnp.bfloat16)
                squares = scale_refs[0][...] + scale_refs[1][...]
                scale = jnp.where(scale_refs[2][...] > 0.5, 1.0, 1.0 / jnp.sqrt(squares + 1e-06))
                scale_ref[...] = down(scale)

        for n, (at, length) in enumerate(spans):
            own_ref, sent_ref, arrived_ref = part_refs[3 * n : 3 * n + 3]

            @pl.when((step >= at) & (step < at + length))
            def _(own_ref=own_ref, sent_ref=sent_ref, arrived_ref=arrived_ref):
                total = own_ref[...].astype(jnp.float32) + sent_ref[...].astype(jnp.float32)
                total = total + arrived_ref[...].astype(jnp.float32)
                product = None
                for p in range(panels):
                    panel = jnp.concatenate([piece_refs[k][p] for k in range(slots)], axis=1)
                    value = lax.dot_general(
                        coef_ref[:, p * order : (p + 1) * order], panel, NT, preferred_element_type=jnp.float32
                    )
                    product = value if product is None else product + value
                scale = jnp.concatenate([scale_ref[...]] * (tile // LANES), axis=1)
                out_ref[...] = ((total - product) * scale).astype(jnp.bfloat16)

    whole = lambda a: pl.BlockSpec(a.shape, lambda i, sc: (0,) * a.ndim)
    in_specs, args = [], []
    for (own, sent, arrived, lane), (at, length) in zip(parts, spans):
        in_specs += [
            block_spec(count, tile, at, length, lane=lane // tile),
            block_spec(count, tile, at, length, row=1, lane=lane // tile),
            block_spec(count, tile, at, length),
        ]
        args += [own, sent, arrived]
    in_specs += [pl.BlockSpec((panels, tile, wide), lambda i, sc: (0, first + i, 0))] * slots
    in_specs += [whole(a) for a in (*coefs, *scales)]
    args += [*pieces, *coefs, *scales]
    out_specs = [pl.BlockSpec((count, tile), lambda i, sc: (0, first + i))]
    out_shape = [jax.ShapeDtypeStruct((count, total_rows), jnp.bfloat16)]
    scratch, aliases = [], {}
    if leads:
        out_specs += [
            pl.BlockSpec((count, panels * order), lambda i, sc: (0, 0)),
            pl.BlockSpec((count, LANES), lambda i, sc: (0, 0)),
        ]
        out_shape += [
            jax.ShapeDtypeStruct((count, panels * order), jnp.bfloat16),
            jax.ShapeDtypeStruct((count, LANES), jnp.float32),
        ]
        scratch = [pltpu.VMEM((count, panels * order), jnp.float32)]
    else:
        in_specs.append(pl.BlockSpec(memory_space=pl.ANY))
        args.append(partial)
        aliases = {len(args): 0}
    return pl.pallas_call(
        kernel,
        grid_spec=pltpu.PrefetchScalarGridSpec(
            num_scalar_prefetch=1,
            grid=(steps,),
            in_specs=in_specs,
            out_specs=out_specs,
            scratch_shapes=scratch,
        ),
        out_shape=out_shape,
        input_output_aliases=aliases,
        name="finish",
    )(place, *args)


def after(value, *before):
    return lax.optimization_barrier((value, *before))[0]


def per_device(
    old_vectors,
    reflectors,
    triangles,
    pole_sq,
    coupling,
    deflated,
    pole_order,
    anchors,
    root_fraction,
):
    side_index = lax.axis_index("side").astype(jnp.int32)
    row_index = lax.axis_index("row").astype(jnp.int32)
    col_index = lax.axis_index("col").astype(jnp.int32)
    row_count, col_count = lax.axis_size("row"), lax.axis_size("col")
    half_rows, slow = row_count // 2, col_count // 2
    old = old_vectors[0]
    col_width = old.shape[1]
    order_size = pole_sq.shape[0]
    count = anchors.shape[0] // col_count
    panel_local = reflectors[0]
    panels = panel_local.shape[0]
    pairs = [(later, earlier) for later in range(panels) for earlier in range(later)]

    def swap(x, axis, mask):
        size = lax.axis_size(axis)
        return lax.ppermute(x, axis, [(i, i ^ mask) for i in range(size)])

    pieces = [panel_local] + [None] * (col_count - 1)
    pieces[slow] = swap(panel_local, "col", slow)
    for fast in range(1, slow):
        pieces[fast] = swap(panel_local, "col", fast)
        pieces[slow + fast] = swap(pieces[slow], "col", fast)

    first_column = row_index // half_rows * (order_size // 2) + col_index * col_width
    place = jnp.stack([first_column, side_index])
    here = jnp.stack([col_index, row_index])
    col_tables = column_tables(place, pole_order, pole_sq, coupling, deflated, col_width)
    tables = [x.reshape(order_size // LANES, LANES) for x in (pole_sq, deflated, pole_order)]
    anchors3 = anchors.reshape(col_count, 1, count)
    fraction3 = root_fraction.reshape(col_count, 1, count)
    slots = [k + s for s in range(1, slow) for k in (slow, 0)] + [slow, 0]
    mix, squares, dead = mixing_rows(place, col_index, slots, anchors3, fraction3, tables, col_tables)
    half_squares = squares[-1]
    for n, k in enumerate(slots[:-1]):
        half_squares = half_squares + swap(squares[n], "col", k)
    other_squares = swap(half_squares, "row", half_rows)

    size = old.shape[0]
    chunk = size // 4
    far, own, near = [], [], []
    for n in range(4):
        sent, keep_far, keep_own = merge(mix, old, n * chunk, chunk, (count, count))
        got = None
        for fast in range(1, slow):
            part = swap(sent[(fast - 1) * 2 * count : fast * 2 * count], "col", fast)
            got = part if got is None else got + part
        far.append(keep_far)
        own.append(keep_own)
        near.append(got)

    def far_sum(n, lane, length):
        lanes = slice(lane, lane + length)
        return far[n][:, lanes] + near[n][:count, lanes]

    gram = panel_products(here, pieces, row_count, pairs)
    half = chunk // 2
    spans = [(0, 0, chunk), (1, 0, chunk), (2, 0, half), (2, half, half), (3, 0, half), (3, half, half)]
    whole_far = [far_sum(n, 0, chunk) for n in range(4)]
    early = 3
    cut = [whole_far[n] if length == chunk else whole_far[n][:, lane : lane + length] for n, lane, length in spans]
    arrived = []
    for n in range(early):
        arrived.append(swap(cut[n], "col", slow))
    (acc,) = project(
        here, [(whole_far[n], own[n], near[n]) for n in range(3)], 0, pieces, row_count, None, False
    )
    far_proj, own_proj = project(
        here, [(whole_far[3], own[3], near[3])], 3 * chunk, pieces, row_count, acc, True
    )

    gram_sum = gram[0].astype(jnp.float32)
    far_total = far_proj[0].astype(jnp.float32)
    shares = [own_proj[0]]
    for t in range(1, row_count):
        gram_sum = gram_sum + swap(gram[t], "row", t).astype(jnp.float32)
        far_total = far_total + swap(far_proj[t], "row", t).astype(jnp.float32)
    far_total = far_total.astype(jnp.bfloat16)
    for t in range(1, row_count):
        shares.append(swap(own_proj[t], "row", t))
    gram_sum = gram_sum.astype(jnp.bfloat16)
    gram_rows = jnp.stack([gram_sum] + [swap(gram_sum, "row", t) for t in range(1, row_count)])
    grams = [None] * col_count
    grams[0], grams[slow] = gram_rows, swap(gram_rows, "col", slow)
    for fast in range(1, slow):
        grams[fast] = swap(gram_rows, "col", fast)
        grams[slow + fast] = swap(grams[slow], "col", fast)
    shares.append(swap(far_total, "col", slow))
    for n in range(early, len(spans)):
        arrived.append(swap(after(cut[n], far_total), "col", slow))
    coef = coefficients(here, shares, grams, triangles[0], pairs)
    coefs = [coef] + [swap(coef, "row", t) for t in range(1, row_count)]

    def part_of(m):
        n, lane, _ = spans[m]
        return (own[n], near[n], arrived[m], lane)

    starts = [n * chunk + lane for n, lane, _ in spans]
    result, coef_all, scale_all = finish(
        here, [part_of(m) for m in range(4)], 0, pieces, coefs, [half_squares, other_squares, dead[-1]]
    )
    for m in (4, 5):
        (result,) = finish(here, [part_of(m)], starts[m], pieces, [coef_all], [scale_all], result)
    return result[None]


def solution(mesh):
    in_specs = (
        P("side", "row", "col"),
        P("side", None, "row", "col"),
        P("side", None, None, None),
        P(),
        P(),
        P(),
        P(),
        P(),
        P(),
    )
    out_specs = P("side", "col", "row")
    return jax.shard_map(per_device, mesh=mesh, in_specs=in_specs, out_specs=out_specs, check_vma=False)
```

```python
import math

import jax
import jax.numpy as jnp
from jax import lax
from jax.experimental import pallas as pl
from jax.experimental.pallas import tpu as pltpu
from jax.sharding import PartitionSpec as P


LANES = 128
HIGHEST = lax.Precision.HIGHEST
NT = (((1,), (1,)), ((), ()))
TN = (((0,), (0,)), ((), ()))


def tile_of(size, want):
    tile = min(size, want)
    while size % tile:
        tile //= 2
    return tile


def split3(x):
    first = x.astype(jnp.bfloat16).astype(jnp.float32)
    rest = x - first
    second = rest.astype(jnp.bfloat16).astype(jnp.float32)
    return first, second, rest - second


def add_up(step, total_ref, value):
    @pl.when(step == 0)
    def _():
        total_ref[...] = value

    @pl.when(step > 0)
    def _():
        total_ref[...] += value


def column_kernel(place_ref, order_ref, sq_ref, coupling_ref, deflated_ref, out_sq_ref, out_num_ref, acc_ref):
    step = pl.program_id(0)

    rows = out_sq_ref.shape[0]
    chunk = order_ref.shape[1]
    local = order_ref[...] - place_ref[0]
    short = lambda x, height: jnp.broadcast_to(x.astype(jnp.float32).astype(jnp.bfloat16), (height, chunk))
    count_up = lambda height: short(lax.broadcasted_iota(jnp.int32, (height, chunk), 0), height)
    zero = jnp.zeros((), jnp.bfloat16)
    in_row = short(local >> 7, rows) == count_up(rows)
    in_lane = jnp.where(short(local & 127, LANES) == count_up(LANES), jnp.ones((), jnp.bfloat16), zero)
    num = (1 - deflated_ref[...]).astype(jnp.float32) * coupling_ref[...]
    parts = [
        jnp.where(in_row, short(part, rows), zero)
        for part in split3(sq_ref[...]) + split3(num)
    ]
    add_up(
        step,
        acc_ref,
        lax.dot_general(
            jnp.concatenate(parts, axis=0),
            in_lane,
            NT,
            preferred_element_type=jnp.float32,
        ),
    )

    @pl.when(step == pl.num_programs(0) - 1)
    def _():
        picked = [acc_ref[i * rows : (i + 1) * rows] for i in range(6)]
        col_sq = (picked[0] + picked[1]) + picked[2]
        weight = jnp.where(place_ref[1] == 0, jnp.ones_like(col_sq), jnp.sqrt(col_sq))
        out_sq_ref[...] = col_sq
        out_num_ref[...] = ((picked[3] + picked[4]) + picked[5]) * weight


def column_tables(place, pole_order, pole_sq, coupling, deflated, col_width):
    order_size = pole_order.shape[0]
    rows = col_width // LANES
    chunk = tile_of(order_size, 16384)
    row_spec = pl.BlockSpec((1, chunk), lambda i, place: (0, i))
    out_spec = pl.BlockSpec((rows, LANES), lambda i, place: (0, 0))
    return pl.pallas_call(
        column_kernel,
        grid_spec=pltpu.PrefetchScalarGridSpec(
            num_scalar_prefetch=1,
            grid=(order_size // chunk,),
            in_specs=[row_spec] * 4,
            out_specs=[out_spec] * 2,
            scratch_shapes=[pltpu.VMEM((6 * rows, LANES), jnp.float32)],
        ),
        out_shape=[jax.ShapeDtypeStruct((rows, LANES), jnp.float32)] * 2,
        name="columns",
    )(place, *(x.reshape(1, order_size) for x in (pole_order, pole_sq, coupling, deflated)))


def down(row, height=LANES):
    return jnp.broadcast_to(row, (height, row.shape[1])).T


def mixing_kernel(place_ref, anchors_ref, fraction_ref, pole_ref, deflated_ref, order_ref, sq_ref, num_ref,
                  mix_ref, squares_ref, dead_ref):
    count = anchors_ref.shape[2]
    anchor = anchors_ref[0]

    def lookup(index, tables):
        table_rows = tables.shape[0]
        onehot = jnp.where(
            lax.broadcasted_iota(jnp.int32, (table_rows, count), 0)
            == jnp.broadcast_to(index >> 7, (table_rows, count)),
            1.0,
            0.0,
        )
        found = lax.dot_general(tables, onehot, TN, precision=HIGHEST, preferred_element_type=jnp.float32)
        mask = lax.broadcasted_iota(jnp.int32, (LANES, count), 0) == jnp.broadcast_to(index & 127, (LANES, count))
        return [
            jnp.sum(jnp.where(mask, found[i : i + LANES], 0.0), axis=0, keepdims=True)
            for i in range(0, found.shape[0], LANES)
        ]

    poles = pole_ref[...]
    tables = jnp.concatenate(
        [poles, deflated_ref[...].astype(jnp.float32), order_ref[...].astype(jnp.float32)], axis=1
    )
    anchor_sq, dead, target = lookup(anchor, tables)
    (next_sq,) = lookup(anchor + 1, poles)
    dead_ref[0] = dead
    anchor_col = down(anchor_sq)
    shift_col = down(fraction_ref[0] * (next_sq - anchor_sq))
    dead_col = down(dead)
    target_col = down(target - place_ref[0].astype(jnp.float32))
    block = tile_of(count, 64)
    chunks = sq_ref.shape[0]
    sums = []
    for start in range(0, count, block):
        part = slice(start, start + block)
        base, shift = anchor_col[part], shift_col[part]
        is_dead, goal = dead_col[part] > 0.5, target_col[part]
        lane = lax.broadcasted_iota(jnp.int32, (block, LANES), 1).astype(jnp.float32)

        def body(c, total, part=part, base=base, shift=shift, is_dead=is_dead, goal=goal, lane=lane):
            col_sq = sq_ref[pl.ds(c, 1), :]
            den = (col_sq - base) - shift
            secular = num_ref[pl.ds(c, 1), :] / den
            first = c * LANES
            onehot = jnp.where(lane + first.astype(jnp.float32) == goal, 1.0, 0.0)
            mix_ref[part, pl.ds(pl.multiple_of(first, LANES), LANES)] = jnp.where(is_dead, onehot, secular).astype(
                jnp.bfloat16
            )
            return total + secular * secular

        sums.append(lax.fori_loop(0, chunks, body, jnp.zeros((block, LANES), jnp.float32), unroll=2))
    total = jnp.concatenate(sums, axis=0)
    squares_ref[0] = jnp.sum(total.T, axis=0, keepdims=True)


def mixing_rows(place, slots, anchors3, fraction3, tables, col_tables):
    count = anchors3.shape[2]
    rows = col_tables[0].shape[0]
    width = rows * LANES

    def pick(i, sc):
        return (sc[4 + i], 0, 0)

    row_spec = pl.BlockSpec((1, 1, count), pick)
    whole = lambda a: pl.BlockSpec(a.shape, lambda i, sc: (0,) * a.ndim)
    out_row = pl.BlockSpec((1, 1, count), lambda i, sc: (i, 0, 0))
    return pl.pallas_call(
        mixing_kernel,
        grid_spec=pltpu.PrefetchScalarGridSpec(
            num_scalar_prefetch=1,
            grid=(len(slots),),
            in_specs=[row_spec, row_spec] + [whole(t) for t in tables] + [whole(t) for t in col_tables],
            out_specs=[pl.BlockSpec((count, width), lambda i, sc: (i, 0)), out_row, out_row],
        ),
        out_shape=[
            jax.ShapeDtypeStruct((len(slots) * count, width), jnp.bfloat16),
            jax.ShapeDtypeStruct((len(slots), 1, count), jnp.float32),
            jax.ShapeDtypeStruct((len(slots), 1, count), jnp.float32),
        ],
        name="mixing",
    )(place, anchors3, fraction3, *tables, *col_tables)


def merge(mix, old, start, size, kept):
    total, depth = mix.shape
    rows = tile_of(math.gcd(size, start) if start else size, 512)
    sent = total - kept[0] - kept[1]
    splits = [(0, sent), (sent, kept[0]), (sent + kept[0], kept[1])]
    first = start // rows

    def kernel(mix_ref, old_ref, *outs):
        value = lax.dot_general(mix_ref[...], old_ref[...], NT, preferred_element_type=jnp.float32)
        for (at, length), out in zip(splits, outs):
            out[...] = value[at : at + length].astype(jnp.bfloat16)

    return pl.pallas_call(
        kernel,
        grid=(size // rows,),
        in_specs=[
            pl.BlockSpec((total, depth), lambda i: (0, 0), pipeline_mode=pl.Buffered(1)),
            pl.BlockSpec((rows, depth), lambda i: (first + i, 0)),
        ],
        out_specs=[pl.BlockSpec((length, rows), lambda i: (0, i)) for _, length in splits],
        out_shape=[jax.ShapeDtypeStruct((length, size), jnp.bfloat16) for _, length in splits],
        compiler_params=pltpu.CompilerParams(vmem_limit_bytes=40 * 2**20),
        name="merge",
    )(mix, old)


def ranges(parts, tile):
    found, at = [], 0
    for part in parts:
        found.append((at, part // tile))
        at += part // tile
    return found, at


def block_spec(height, tile, at, steps, row=0, lane=0):
    return pl.BlockSpec((height, tile), lambda i, sc: (row, lane + jnp.clip(i - at, 0, steps - 1)))


def project(place, parts, start, pieces, row_count, init=None, last=True):
    slots, (panels, _, wide) = len(pieces), pieces[0].shape
    count = parts[0][0].shape[0]
    order = slots * wide
    tile = tile_of(parts[0][0].shape[1], 2048)
    spans, steps = ranges([part[0].shape[1] for part in parts], tile)
    sub = count // row_count
    first = start // tile
    n_init = 0 if init is None else 1

    def kernel(sc_ref, *refs):
        part_refs, refs = refs[: 3 * len(parts)], refs[3 * len(parts) :]
        piece_refs, refs = refs[:slots], refs[slots:]
        init_refs, refs = refs[:n_init], refs[n_init:]
        outs, acc_ref = refs[:-1], refs[-1]
        step = pl.program_id(0)
        for n, (at, length) in enumerate(spans):
            far_ref, own_ref, sent_ref = part_refs[3 * n : 3 * n + 3]

            @pl.when((step >= at) & (step < at + length))
            def _(far_ref=far_ref, own_ref=own_ref, sent_ref=sent_ref):
                own = own_ref[...].astype(jnp.float32) + sent_ref[...].astype(jnp.float32)
                both = jnp.concatenate([far_ref[...], own.astype(jnp.bfloat16)], axis=0)
                for p in range(panels):
                    panel = jnp.concatenate([piece_refs[k][p] for k in range(slots)], axis=1)
                    value = jnp.dot(both, panel, preferred_element_type=jnp.float32)
                    if init is None:
                        add_up(step, acc_ref.at[p], value)
                    else:

                        @pl.when(step == 0)
                        def _(p=p, value=value):
                            acc_ref[p] = init_refs[0][p] + value

                        @pl.when(step > 0)
                        def _(p=p, value=value):
                            acc_ref[p] += value

        @pl.when(step == pl.num_programs(0) - 1)
        def _():
            if not last:
                outs[0][...] = acc_ref[...]
                return
            col, row = sc_ref[2], sc_ref[3]
            for t in range(row_count):
                at = pl.multiple_of((row ^ t) * sub, sub)
                for p in range(panels):
                    for k in range(slots):
                        lanes = pl.ds(pl.multiple_of(p * order + (col ^ k) * wide, wide), wide)
                        cols = slice(k * wide, (k + 1) * wide)
                        outs[0][t, :, lanes] = acc_ref[p, pl.ds(at, sub), cols].astype(jnp.bfloat16)
                        outs[1][t, :, lanes] = acc_ref[p, pl.ds(at + count, sub), cols].astype(jnp.bfloat16)

    acc_shape = (panels, 2 * count, order)
    if last:
        out_shapes = [jax.ShapeDtypeStruct((row_count, sub, panels * order), jnp.bfloat16)] * 2
    else:
        out_shapes = [jax.ShapeDtypeStruct(acc_shape, jnp.float32)]
    in_specs = []
    for at, length in spans:
        in_specs += [block_spec(count, tile, at, length)] * 2 + [block_spec(count, tile, at, length, row=1)]
    in_specs += [pl.BlockSpec((panels, tile, wide), lambda i, sc: (0, first + i, 0))] * slots
    if init is not None:
        in_specs += [pl.BlockSpec(acc_shape, lambda i, sc: (0, 0, 0), pipeline_mode=pl.Buffered(1))]
    return pl.pallas_call(
        kernel,
        grid_spec=pltpu.PrefetchScalarGridSpec(
            num_scalar_prefetch=1,
            grid=(steps,),
            in_specs=in_specs,
            out_specs=[pl.BlockSpec(s.shape, lambda i, sc: (0, 0, 0)) for s in out_shapes],
            scratch_shapes=[pltpu.VMEM(acc_shape, jnp.float32)],
        ),
        out_shape=out_shapes,
        name="project",
    )(place, *(a for part in parts for a in part), *pieces, *(() if init is None else (init,)))


def panel_products(place, pieces, row_count, pairs):
    slots, (panels, size, wide) = len(pieces), pieces[0].shape
    order = slots * wide
    tile = tile_of(size, 2048)
    sub_gram = order // row_count
    needed = [(k, p) for k in range(slots) for p in range(panels) if k == 0 or p > 0]

    def kernel(sc_ref, *refs):
        panel_refs = dict(zip(needed, refs))
        gram_out, gram_ref, nat_ref = refs[len(needed) :]
        step = pl.program_id(0)
        for n, (later, earlier) in enumerate(pairs):
            panel = jnp.concatenate([panel_refs[k, later][0] for k in range(slots)], axis=1)
            product = lax.dot_general(
                panel_refs[0, earlier][0], panel, TN, preferred_element_type=jnp.float32
            )
            add_up(step, gram_ref.at[n], product)

        @pl.when(step == pl.num_programs(0) - 1)
        def _():
            col, row = sc_ref[2], sc_ref[3]
            for n in range(len(pairs)):
                for k in range(slots):
                    at = pl.multiple_of((col ^ k) * wide, wide)
                    nat_ref[pl.ds(at, wide), :] = gram_ref[n, :, k * wide : (k + 1) * wide].T
                for t in range(row_count):
                    at = pl.multiple_of((row ^ t) * sub_gram, sub_gram)
                    gram_out[t, n] = nat_ref[pl.ds(at, sub_gram), :].astype(jnp.bfloat16)

    out_shape = jax.ShapeDtypeStruct((row_count, len(pairs), sub_gram, wide), jnp.bfloat16)
    return pl.pallas_call(
        kernel,
        grid_spec=pltpu.PrefetchScalarGridSpec(
            num_scalar_prefetch=1,
            grid=(size // tile,),
            in_specs=[pl.BlockSpec((1, tile, wide), lambda i, sc, p=p: (p, i, 0)) for _, p in needed],
            out_specs=pl.BlockSpec(out_shape.shape, lambda i, sc: (0, 0, 0, 0)),
            scratch_shapes=[
                pltpu.VMEM((len(pairs), wide, order), jnp.float32),
                pltpu.VMEM((order, wide), jnp.float32),
            ],
        ),
        out_shape=out_shape,
        name="gram",
    )(place, *(pieces[k] for k, _ in needed))


def coefficients(place, shares, grams, triangles, pairs):
    panels, order = triangles.shape[0], triangles.shape[1]
    sub = shares[0].shape[0]
    slots = len(grams)
    row_count, _, sub_gram, wide = grams[0].shape

    def kernel(sc_ref, *refs):
        share_refs = refs[: len(shares)]
        gram_refs = refs[len(shares) : len(shares) + slots]
        tri_ref, out_ref, nat_ref = refs[len(shares) + slots :]
        col, row = sc_ref[2], sc_ref[3]
        for n in range(len(pairs)):
            for k in range(slots):
                for t in range(row_count):
                    rows = pl.ds(pl.multiple_of((row ^ t) * sub_gram, sub_gram), sub_gram)
                    lanes = pl.ds(pl.multiple_of((col ^ k) * wide, wide), wide)
                    nat_ref[n, rows, lanes] = gram_refs[k][t, n].astype(jnp.float32)
        total = share_refs[0][...].astype(jnp.float32)
        for ref in share_refs[1:]:
            total = total + ref[...].astype(jnp.float32)
        keep = lax.broadcasted_iota(jnp.int32, (order, order), 0) <= lax.broadcasted_iota(
            jnp.int32, (order, order), 1
        )
        found = [None] * panels
        for p in reversed(range(panels)):
            projected = total[:, p * order : (p + 1) * order]
            for later in range(p + 1, panels):
                gram = nat_ref[pairs.index((later, p))].astype(jnp.bfloat16)
                projected = projected - jnp.dot(found[later], gram, preferred_element_type=jnp.float32)
            upper = jnp.where(keep, tri_ref[p], 0.0)
            found[p] = lax.dot_general(
                projected, upper, NT, precision=HIGHEST, preferred_element_type=jnp.float32
            ).astype(jnp.bfloat16)
            out_ref[:, p * order : (p + 1) * order] = found[p]

    whole = lambda a: pl.BlockSpec(a.shape, lambda i, sc: (0,) * a.ndim)
    args = [*shares, *grams, triangles]
    return pl.pallas_call(
        kernel,
        grid_spec=pltpu.PrefetchScalarGridSpec(
            num_scalar_prefetch=1,
            grid=(1,),
            in_specs=[whole(a) for a in args],
            out_specs=pl.BlockSpec((sub, panels * order), lambda i, sc: (0, 0)),
            scratch_shapes=[pltpu.VMEM((len(pairs), order, order), jnp.float32)],
        ),
        out_shape=jax.ShapeDtypeStruct((sub, panels * order), jnp.bfloat16),
        name="coefficients",
    )(place, *args)


def finish(place, parts, start, pieces, coefs, scales, partial=None):
    slots, (panels, total_rows, wide) = len(pieces), pieces[0].shape
    count = parts[0][0].shape[0]
    order = slots * wide
    leads = partial is None
    tile = min([tile_of(part[2].shape[1], 2048) for part in parts])
    spans, steps = ranges([part[2].shape[1] for part in parts], tile)
    first = start // tile
    n_coef, n_scale = len(coefs), len(scales)

    def kernel(sc_ref, *refs):
        part_refs, refs = refs[: 3 * len(parts)], refs[3 * len(parts) :]
        piece_refs, refs = refs[:slots], refs[slots:]
        coef_refs, refs = refs[:n_coef], refs[n_coef:]
        scale_refs, refs = refs[:n_scale], refs[n_scale:]
        if leads:
            out_ref, coef_ref, scale_ref, wide_ref = refs
        else:
            out_ref, coef_ref, scale_ref = refs[1], coef_refs[0], scale_refs[0]
        step = pl.program_id(0)

        if leads:

            @pl.when(step == 0)
            def _():
                col, row = sc_ref[2], sc_ref[3]
                sub = coef_refs[0].shape[0]
                for t in range(n_coef):
                    rows = pl.ds(pl.multiple_of((row ^ t) * sub, sub), sub)
                    for p in range(panels):
                        for k in range(slots):
                            lanes = pl.ds(pl.multiple_of(p * order + (col ^ k) * wide, wide), wide)
                            at = p * order + k * wide
                            wide_ref[rows, at : at + wide] = coef_refs[t][:, lanes].astype(jnp.float32)
                coef_ref[...] = wide_ref[...].astype(jnp.bfloat16)
                squares = scale_refs[0][...] + scale_refs[1][...]
                scale = jnp.where(scale_refs[2][...] > 0.5, 1.0, 1.0 / jnp.sqrt(squares + 1e-06))
                scale_ref[...] = down(scale)

        for n, (at, length) in enumerate(spans):
            own_ref, sent_ref, arrived_ref = part_refs[3 * n : 3 * n + 3]

            @pl.when((step >= at) & (step < at + length))
            def _(own_ref=own_ref, sent_ref=sent_ref, arrived_ref=arrived_ref):
                total = own_ref[...].astype(jnp.float32) + sent_ref[...].astype(jnp.float32)
                total = total + arrived_ref[...].astype(jnp.float32)
                product = None
                for p in range(panels):
                    panel = jnp.concatenate([piece_refs[k][p] for k in range(slots)], axis=1)
                    value = lax.dot_general(
                        coef_ref[:, p * order : (p + 1) * order], panel, NT, preferred_element_type=jnp.float32
                    )
                    product = value if product is None else product + value
                scale = jnp.concatenate([scale_ref[...]] * (tile // LANES), axis=1)
                out_ref[...] = ((total - product) * scale).astype(jnp.bfloat16)

    whole = lambda a: pl.BlockSpec(a.shape, lambda i, sc: (0,) * a.ndim)
    in_specs, args = [], []
    for (own, sent, arrived, lane), (at, length) in zip(parts, spans):
        in_specs += [
            block_spec(count, tile, at, length, lane=lane // tile),
            block_spec(count, tile, at, length, row=1, lane=lane // tile),
            block_spec(count, tile, at, length),
        ]
        args += [own, sent, arrived]
    in_specs += [pl.BlockSpec((panels, tile, wide), lambda i, sc: (0, first + i, 0))] * slots
    in_specs += [whole(a) for a in (*coefs, *scales)]
    args += [*pieces, *coefs, *scales]
    out_specs = [pl.BlockSpec((count, tile), lambda i, sc: (0, first + i))]
    out_shape = [jax.ShapeDtypeStruct((count, total_rows), jnp.bfloat16)]
    scratch, aliases = [], {}
    if leads:
        out_specs += [
            pl.BlockSpec((count, panels * order), lambda i, sc: (0, 0)),
            pl.BlockSpec((count, LANES), lambda i, sc: (0, 0)),
        ]
        out_shape += [
            jax.ShapeDtypeStruct((count, panels * order), jnp.bfloat16),
            jax.ShapeDtypeStruct((count, LANES), jnp.float32),
        ]
        scratch = [pltpu.VMEM((count, panels * order), jnp.float32)]
    else:
        in_specs.append(pl.BlockSpec(memory_space=pl.ANY))
        args.append(partial)
        aliases = {len(args): 0}
    return pl.pallas_call(
        kernel,
        grid_spec=pltpu.PrefetchScalarGridSpec(
            num_scalar_prefetch=1,
            grid=(steps,),
            in_specs=in_specs,
            out_specs=out_specs,
            scratch_shapes=scratch,
        ),
        out_shape=out_shape,
        input_output_aliases=aliases,
        name="finish",
    )(place, *args)


def after(value, *before):
    return lax.optimization_barrier((value, *before))[0]


def per_device(
    old_vectors,
    reflectors,
    triangles,
    pole_sq,
    coupling,
    deflated,
    pole_order,
    anchors,
    root_fraction,
):
    side_index = lax.axis_index("side").astype(jnp.int32)
    row_index = lax.axis_index("row").astype(jnp.int32)
    col_index = lax.axis_index("col").astype(jnp.int32)
    row_count, col_count = lax.axis_size("row"), lax.axis_size("col")
    half_rows, slow = row_count // 2, col_count // 2
    old = old_vectors[0]
    col_width = old.shape[1]
    order_size = pole_sq.shape[0]
    count = anchors.shape[0] // col_count
    panel_local = reflectors[0]
    panels = panel_local.shape[0]
    pairs = [(later, earlier) for later in range(panels) for earlier in range(later)]

    def swap(x, axis, mask):
        size = lax.axis_size(axis)
        return lax.ppermute(x, axis, [(i, i ^ mask) for i in range(size)])

    pieces = [panel_local] + [None] * (col_count - 1)
    pieces[slow] = swap(panel_local, "col", slow)
    for fast in range(1, slow):
        pieces[fast] = swap(panel_local, "col", fast)
        pieces[slow + fast] = swap(pieces[slow], "col", fast)

    first_column = row_index // half_rows * (order_size // 2) + col_index * col_width
    slots = [k + f for f in range(1, slow) for k in (slow, 0)] + [slow, 0]
    place = jnp.stack([first_column, side_index, col_index, row_index] + [col_index ^ k for k in slots])
    col_tables = column_tables(place, pole_order, pole_sq, coupling, deflated, col_width)
    tables = [x.reshape(order_size // LANES, LANES) for x in (pole_sq, deflated, pole_order)]
    anchors3 = anchors.reshape(col_count, 1, count)
    fraction3 = root_fraction.reshape(col_count, 1, count)
    mix, squares, dead = mixing_rows(place, slots, anchors3, fraction3, tables, col_tables)
    half_squares = squares[-1]
    for n, k in enumerate(slots[:-1]):
        half_squares = half_squares + swap(squares[n], "col", k)
    other_squares = swap(half_squares, "row", half_rows)

    size = old.shape[0]
    lengths = [size // 4, size // 2, size // 4]
    starts = [sum(lengths[:n]) for n in range(3)]
    far, own, near = [], [], []
    for n in range(3):
        sent, keep_far, keep_own = merge(mix, old, starts[n], lengths[n], (count, count))
        got = None
        for fast in range(1, slow):
            part = swap(sent[(fast - 1) * 2 * count : fast * 2 * count], "col", fast)
            got = part if got is None else got + part
        far.append(keep_far + got[:count])
        own.append(keep_own)
        near.append(got)
    gram = panel_products(place, pieces, row_count, pairs)
    arrived = []
    for n in range(2):
        arrived.append(swap(far[n], "col", slow))
    far_proj, own_proj = project(place, list(zip(far, own, near)), 0, pieces, row_count)

    gram_sum = gram[0].astype(jnp.float32)
    far_total = far_proj[0].astype(jnp.float32)
    shares = [own_proj[0]]
    for t in range(1, row_count):
        gram_sum = gram_sum + swap(gram[t], "row", t).astype(jnp.float32)
        far_total = far_total + swap(far_proj[t], "row", t).astype(jnp.float32)
    far_total = far_total.astype(jnp.bfloat16)
    for t in range(1, row_count):
        shares.append(swap(own_proj[t], "row", t))
    gram_sum = gram_sum.astype(jnp.bfloat16)
    gathered = [gram_sum]
    for t in range(1, row_count):
        gathered.append(swap(gram_sum, "row", t))
    gram_rows = jnp.stack(gathered)
    grams = [None] * col_count
    grams[0] = gram_rows
    grams[slow] = swap(gram_rows, "col", slow)
    for fast in range(1, slow):
        grams[fast] = swap(gram_rows, "col", fast)
        grams[slow + fast] = swap(grams[slow], "col", fast)
    shares.append(swap(far_total, "col", slow))
    arrived.append(swap(after(far[2], far_total), "col", slow))
    coef = coefficients(place, shares, grams, triangles[0], pairs)
    coefs = [coef] + [swap(coef, "row", t) for t in range(1, row_count)]

    parts = [(*part, 0) for part in zip(own, near, arrived)]
    norms = [half_squares, other_squares, dead[-1]]
    return finish(place, parts, 0, pieces, coefs, norms)[0][None]


def solution(mesh):
    in_specs = (
        P("side", "row", "col"),
        P("side", None, "row", "col"),
        P("side", None, None, None),
        P(),
        P(),
        P(),
        P(),
        P(),
        P(),
    )
    out_specs = P("side", "col", "row")
    return jax.shard_map(per_device, mesh=mesh, in_specs=in_specs, out_specs=out_specs, check_vma=False)
```
